32 devices in a mesh: dp: 4 (over x, core), query: 8 (over z, y).
Axes of the slice: x: 2, y: 2, z: 4, core: 2. Of those that a mesh axis runs over, the one named last changes fastest.
Arguments:
- corpus: bfloat16 [131072, 1024], P(('dp', 'query')), may hold values from -6 to 6
- queries: float32 [512, 1024], P('query'), may hold values from -800 to 800
- cand_ids: int32 [32, 512, 8], P(('dp', 'query')), may hold values from 0 to 4095
- cand_counts: int32 [32, 512], P(('dp', 'query')), may hold values from 1 to 8
Outputs:
- log_total: float32 [512], P('query')
- pooled: float32 [512, 1024], P('query')
The draws below stay inside these ranges and needn't reach their ends.
All inputs are finite; a program needn't handle non-finite values.
Results may differ from the reference program's by a relative error of at most 0.0003.
Values may be sent and summed in bfloat16 or wider, within the bound.
A program may use at most 128 MiB of HBM per device.

```python
import jax
import jax.numpy as jnp
from jax import lax

D = 1024
R_DEV = 4096
C = 8
QUERIES = 512
ROWS = 131072
DEVICES = 32


def draw_queries(key, part):
    base = jnp.clip(jax.random.normal(jax.random.fold_in(key, 11), (QUERIES, D), jnp.float32), -4.0, 4.0)
    return base


def place_ends(array, own_key, least, top_value):
    place = [jax.random.randint(jax.random.fold_in(own_key, axis), (), 0, length) for axis, length in enumerate(array.shape)]
    main_axis = array.shape.index(max(array.shape))
    neighbour = place[:main_axis] + [(place[main_axis] + 1) % array.shape[main_axis]] + place[main_axis + 1:]
    return array.at[tuple(place)].set(least).at[tuple(neighbour)].set(top_value)


def steps_of(key, dims, split, smallest, high):
    loudness = 1.0
    for position, shards_of in split:
        draws = jax.random.uniform(jax.random.fold_in(jax.random.fold_in(key, 6), position), (shards_of,), jnp.float32, smallest / len(split), high / len(split))
        loudness = loudness * jnp.repeat(jnp.exp(draws), dims[position] // shards_of).reshape((-1,) + (1,) * (len(dims) - 1 - position))
    return loudness


def normal_values(stream_key, dims, deviation, bound, split=(), kind=jnp.bfloat16):
    values = deviation * jax.random.normal(stream_key, dims, jnp.float32)
    if split:
        values = values * steps_of(stream_key, dims, split, -0.22, 0.18)
    return jnp.clip(values, -bound, bound).astype(kind)


def setup_inputs(seed: int = 0) -> dict:
    splits = jax.random.split(jax.random.key(seed), 5)
    return {
        "corpus": normal_values(splits[0], (ROWS, D), 1.0, 6.0, ((0, 32),)),
        "queries": draw_queries(jax.random.fold_in(splits[4], 71), 0),
        "cand_ids": place_ends(jax.random.randint(splits[2], (DEVICES, QUERIES, C), 0, R_DEV), jax.random.fold_in(splits[2], 1), 0, R_DEV - 1).astype(jnp.int32),
        "cand_counts": place_ends(jax.random.randint(splits[3], (DEVICES, QUERIES), 1, C + 1), jax.random.fold_in(splits[3], 1), 1, C).astype(jnp.int32),
    }


def reference(corpus, queries, cand_ids, cand_counts):
    shards = corpus.reshape(DEVICES, R_DEV, D)
    inverse_root = jnp.float32(1.0) / jnp.sqrt(jnp.float32(D))
    slot_index = jnp.arange(C, dtype=jnp.int32)

    def absorb(running, inputs):
        best, total, weighted = running
        shard_block, local_ids, counts = inputs
        picked = shard_block[local_ids].astype(jnp.float32)
        scores = jnp.einsum('qcd,qd->qc', picked, queries, precision=lax.Precision.HIGHEST) * inverse_root
        alive_mask = slot_index[None, :] < counts[:, None]
        masked = jnp.where(alive_mask, scores, jnp.float32(-1e+30))
        newbest = jnp.maximum(best, lax.optimization_barrier(jnp.max(masked, axis=1)))
        weights = jnp.where(alive_mask, jnp.exp(masked - newbest[:, None]), jnp.float32(0.0))
        rescale = jnp.exp(best - newbest)
        total = total * rescale + lax.optimization_barrier(jnp.sum(weights, axis=1))
        weighted = weighted * rescale[:, None] + jnp.einsum('qc,qcd->qd', weights, picked, precision=lax.Precision.HIGHEST)
        return ((newbest, total, weighted), None)
    start = (jnp.full((QUERIES,), -1e+30, jnp.float32), jnp.zeros((QUERIES,), jnp.float32), jnp.zeros((QUERIES, D), jnp.float32))
    (best, total, weighted), _ = lax.scan(absorb, start, (shards, cand_ids, cand_counts))
    return (best + jnp.log(total), weighted / total[:, None])
```

```python
import functools

import jax
import jax.numpy as jnp
from jax import lax
from jax.experimental import pallas as pl
from jax.experimental.pallas import tpu as pltpu
from jax.sharding import PartitionSpec as P

MESH = pl.DeviceIdType.MESH
LANES = 128
SUB = 8
NEG = -1e30
CHUNK = 256
SLOTS = 4


def low_bit(k):
    return (k & -k).bit_length() - 1


def halves_combine(a, b, step, mask):
    u = jnp.where(mask, a, b)
    v = jnp.where(mask, b, a)
    return u + pltpu.roll(v, step, 0)


def sub_reduce(x, op):
    for step in (4, 2, 1):
        x = op(x, pltpu.roll(x, step, 0))
    return x


def kernel(
    cfg, ids, counts, q_hbm, corpus_hbm, out_ref, log_ref,
    c32, stage, allq, acc, rcore, rbits, rx, fin,
    stage_sem, own_sem, ag_send, ag_recv, agc_send, agc_recv,
    rc_send, rc_recv, rb_send, rb_recv, rx_send, rx_recv, fin_send, fin_recv,
):
    n, d, half_rows, slots, tiles, rows, inv_root = cfg
    nbits = n.bit_length() - 1
    dbits = d.bit_length() - 1
    me = lax.axis_index("query")
    dp = lax.axis_index("dp")
    core = lax.rem(dp, 2)
    other = 1 - core
    stat = tiles * SUB
    group_rows = (tiles + 1) * SUB
    groups = half_rows // SUB
    piece = groups * group_rows
    qpiece = half_rows * tiles

    def flip(x, bit):
        return x + (1 << bit) - 2 * (1 << bit) * lax.rem(x // (1 << bit), 2)

    def owner(k):
        s = me
        for b in range(nbits):
            if k >> b & 1:
                s = flip(s, b)
        return s

    def q_to(bit):
        return {"query": flip(me, bit)}

    def d_to(bit):
        return {"dp": flip(dp, bit)}

    barrier = pltpu.get_barrier_semaphore()
    for b in range(nbits):
        pl.semaphore_signal(barrier, inc=1, device_id=q_to(b), device_id_type=MESH)
    for b in range(dbits):
        pl.semaphore_signal(barrier, inc=1, device_id=d_to(b), device_id_type=MESH)

    def stage_copy(i, slot):
        return pltpu.make_async_copy(
            corpus_hbm.at[pl.ds(i * CHUNK, CHUNK), :], stage.at[slot], stage_sem.at[slot]
        )

    for i in range(SLOTS):
        stage_copy(i, i).start()

    def q_at(s, half):
        return pl.multiple_of((s * 2 + half) * qpiece, SUB)

    own_copy = pltpu.make_async_copy(
        q_hbm, allq.at[pl.ds(pl.multiple_of(me * (2 * qpiece), SUB), 2 * qpiece), :], own_sem
    )
    own_copy.start()
    pl.semaphore_wait(barrier, nbits + dbits)

    started = []

    def remote(src, dst, send, recv, to):
        copy = pltpu.make_async_remote_copy(
            src_ref=src, dst_ref=dst, send_sem=send, recv_sem=recv,
            device_id=to, device_id_type=MESH,
        )
        copy.start()
        started.append(copy)
        return copy

    def ag_piece(k, half):
        return allq.at[pl.ds(q_at(owner(k), half), qpiece), :]

    def ag_forward(k):
        for b in reversed(range(low_bit(k) if k else nbits)):
            if k:
                src = ag_piece(k, core)
            else:
                src = q_hbm.at[pl.ds(pl.multiple_of(core * qpiece, SUB), qpiece), :]
            j = k | 1 << b
            remote(src, ag_piece(k, core), ag_send.at[j], ag_recv.at[j], q_to(b))
        if k:
            remote(ag_piece(k, core), ag_piece(k, core), agc_send.at[k], agc_recv.at[k], d_to(0))

    def arrived(k, half, send, recv, to):
        pltpu.make_async_remote_copy(
            src_ref=ag_piece(k, half), dst_ref=ag_piece(k, half), send_sem=send.at[k],
            recv_sem=recv.at[k], device_id=to, device_id_type=MESH,
        ).wait_recv()

    def relay(k):
        arrived(k, core, ag_send, ag_recv, q_to(low_bit(k)))
        ag_forward(k)

    ag_forward(0)

    n_chunks = rows // CHUNK
    flat = c32.reshape(rows * tiles, LANES)

    def convert(i, _):
        slot = lax.rem(i, SLOTS)
        stage_copy(i, slot).wait()

        def block(r, _):
            r0 = pl.multiple_of(r * 16, 16)
            to = pl.multiple_of((i * CHUNK + r * 16) * tiles, SUB)
            for j in range(tiles):
                x = stage[slot, pl.ds(r0, 16), j * LANES : (j + 1) * LANES].astype(jnp.float32)
                flat[pl.ds(to + j, SUB, stride=tiles), :] = x[:SUB]
                flat[pl.ds(to + SUB * tiles + j, SUB, stride=tiles), :] = x[SUB:]
            return 0

        lax.fori_loop(0, CHUNK // 16, block, 0)

        @pl.when(i + SLOTS < n_chunks)
        def _():
            stage_copy(i + SLOTS, slot).start()

        return 0

    relays = sorted(range(1, n), key=lambda k: (k.bit_count(), -low_bit(k), k))
    pending = list(relays)
    parts = 4
    for part in range(parts):
        lax.fori_loop(part * n_chunks // parts, (part + 1) * n_chunks // parts, convert, 0)
        if part and pending:
            relay(pending.pop(0))

    sub = lax.broadcasted_iota(jnp.int32, (SUB, LANES), 0)
    lane = lax.broadcasted_iota(jnp.int32, (SUB, LANES), 1)
    masks = {4: sub < 4, 2: lax.rem(sub, 4) < 2, 1: lax.rem(sub, 2) < 1}

    def acc_at(s, half):
        return pl.multiple_of((s * 2 + half) * piece, SUB)

    def compute(k, half):
        s = owner(k)
        q0 = q_at(s, half)
        a0 = acc_at(s, half)
        first = s * (2 * half_rows) + half * half_rows

        def row(index):
            return c32[ids[index]]

        def group(g, _):
            query = first + g * SUB
            weights, stats = [], jnp.zeros((SUB, LANES), jnp.float32)
            for qi in range(SUB):
                at = (query + qi) * slots
                q = allq[pl.ds(pl.multiple_of(q0 + (g * SUB + qi) * tiles, SUB), tiles), :]
                level = [row(at + c) * q for c in range(slots)]
                for step in (1, 2, 4):
                    level = [
                        halves_combine(a, b, step, masks[step])
                        for a, b in zip(level[::2], level[1::2])
                    ]
                score = jnp.sum(level[0], axis=1, keepdims=True) * inv_root
                score = jnp.broadcast_to(score, (SUB, LANES))
                live = sub < counts[query + qi]
                score = jnp.where(live, score, NEG)
                best = sub_reduce(score, jnp.maximum)
                weight = jnp.where(live, jnp.exp(score - best), 0.0)
                total = sub_reduce(weight, jnp.add)
                weights.append(weight)
                stats = jnp.where(sub == qi, jnp.where(lane < LANES // 2, best, total), stats)
            base = pl.multiple_of(a0 + g * group_rows, SUB)
            for qi in range(SUB):
                at = (query + qi) * slots
                terms = [
                    jnp.broadcast_to(weights[qi][c : c + 1, :], (SUB, LANES)) * row(at + c)
                    for c in range(slots)
                ]
                while len(terms) > 1:
                    terms = [a + b for a, b in zip(terms[::2], terms[1::2])]
                acc[pl.ds(base + qi, tiles, stride=SUB), :] = terms[0]
            acc[pl.ds(pl.multiple_of(base + stat, SUB), SUB), :] = stats
            return 0

        lax.fori_loop(0, groups, group, 0)

    def split(x):
        turned = pltpu.roll(x, LANES // 2, 1)
        left = lane < LANES // 2
        return jnp.where(left, x, turned), jnp.where(left, turned, x)

    def merge(k, ref, at, swap=None):
        a0 = acc_at(owner(k), core)

        def group(g, _):
            mine = pl.multiple_of(a0 + g * group_rows, SUB)
            theirs = pl.multiple_of(at + g * group_rows, SUB)

            def load(off):
                x = acc[pl.ds(pl.multiple_of(mine + off, SUB), SUB), :]
                y = ref[pl.ds(pl.multiple_of(theirs + off, SUB), SUB), :]
                if swap is not None:
                    x, y = jnp.where(swap, y, x), jnp.where(swap, x, y)
                return x, y

            x, y = load(stat)
            best_x, total_x = split(x)
            best_y, total_y = split(y)
            best = jnp.maximum(best_x, best_y)
            scale_x = jnp.exp(best_x - best)
            scale_y = jnp.exp(best_y - best)
            total = total_x * scale_x + total_y * scale_y
            acc[pl.ds(pl.multiple_of(mine + stat, SUB), SUB), :] = jnp.where(
                lane < LANES // 2, best, total
            )
            for j in range(tiles):
                x, y = load(j * SUB)
                acc[pl.ds(pl.multiple_of(mine + j * SUB, SUB), SUB), :] = x * scale_x + y * scale_y
            return 0

        lax.fori_loop(0, groups, group, 0)

    def acc_piece(k, half):
        return acc.at[pl.ds(acc_at(owner(k), half), piece), :]

    def slot_of(ref, k):
        return ref.at[pl.ds(k * piece, piece), :]

    core_copies = {}

    def share(k):
        core_copies[k] = remote(
            acc_piece(k, other), slot_of(rcore, k), rc_send.at[k], rc_recv.at[k], d_to(0)
        )

    def finish(k):
        core_copies[k].wait_recv()
        merge(k, rcore, k * piece)
        for b in range(low_bit(k) if k else nbits):
            j = k | 1 << b
            pltpu.make_async_remote_copy(
                src_ref=slot_of(rbits, j), dst_ref=slot_of(rbits, j), send_sem=rb_send.at[j],
                recv_sem=rb_recv.at[j], device_id=q_to(b), device_id_type=MESH,
            ).wait_recv()
            merge(k, rbits, j * piece)
        if k:
            remote(acc_piece(k, core), slot_of(rbits, k), rb_send.at[k], rb_recv.at[k], q_to(low_bit(k)))

    order = [0] + sorted(range(1, n), key=lambda k: (low_bit(k), k.bit_count(), k))
    own_copy.wait()
    late = None
    for k in order:
        while k and k in pending:
            relay(pending.pop(0))
        if k:
            arrived(k, other, agc_send, agc_recv, d_to(0))
        compute(k, other)
        share(k)
        compute(k, core)
        if late:
            finish(late)
        late = k
    finish(late)
    finish(0)

    for b in range(1, dbits):
        pltpu_copy = pltpu.make_async_remote_copy(
            src_ref=acc_piece(0, core), dst_ref=slot_of(rx, b), send_sem=rx_send.at[b],
            recv_sem=rx_recv.at[b], device_id=d_to(b), device_id_type=MESH,
        )
        pltpu_copy.start()
        pltpu_copy.wait()
        upper = jnp.full((SUB, LANES), lax.rem(dp // (1 << b), 2), jnp.int32)
        merge(0, rx, b * piece, swap=upper == 1)

    last = remote(acc_piece(0, core), fin, fin_send, fin_recv, d_to(0))

    def emit(ref, at, half):
        for g in range(groups):
            base = pl.multiple_of(at + g * group_rows, SUB)
            to = pl.multiple_of(half * half_rows + g * SUB, SUB)
            best, total = split(ref[pl.ds(pl.multiple_of(base + stat, SUB), SUB), :])
            log_ref[pl.ds(to, SUB), :] = best + jnp.log(total)
            inverse = 1.0 / total
            for j in range(tiles):
                out_ref[pl.ds(to, SUB), j * LANES : (j + 1) * LANES] = (
                    ref[pl.ds(pl.multiple_of(base + j * SUB, SUB), SUB), :] * inverse
                )

    emit(acc, acc_at(me, core), core)
    last.wait_recv()
    emit(fin, 0, other)
    for copy in started:
        copy.wait_send()


def body(corpus, queries, cand_ids, cand_counts):
    n, d = lax.axis_size("query"), lax.axis_size("dp")
    own, width = queries.shape
    slots = cand_ids.shape[2]
    rows = corpus.shape[0]
    tiles = width // LANES
    half_rows = own // 2
    inv_root = 1.0 / float(width) ** 0.5
    ids = cand_ids.reshape(-1)
    counts = cand_counts.reshape(-1)
    piece = half_rows // SUB * (tiles + 1) * SUB
    qpiece = half_rows * tiles
    dbits = d.bit_length() - 1
    f32 = jnp.float32
    dma = pltpu.SemaphoreType.DMA
    out, logs = pl.pallas_call(
        functools.partial(kernel, (n, d, half_rows, slots, tiles, rows, inv_root)),
        out_shape=(
            jax.ShapeDtypeStruct((own, width), f32),
            jax.ShapeDtypeStruct((own, LANES), f32),
        ),
        in_specs=[
            pl.BlockSpec(memory_space=pltpu.SMEM),
            pl.BlockSpec(memory_space=pltpu.SMEM),
            pl.BlockSpec(memory_space=pl.ANY),
            pl.BlockSpec(memory_space=pl.ANY),
        ],
        out_specs=(pl.BlockSpec(memory_space=pltpu.VMEM), pl.BlockSpec(memory_space=pltpu.VMEM)),
        scratch_shapes=[
            pltpu.VMEM((rows, tiles, LANES), f32),
            pltpu.VMEM((SLOTS, CHUNK, width), corpus.dtype),
            pltpu.VMEM((n * 2 * qpiece, LANES), f32),
            pltpu.VMEM((n * 2 * piece, LANES), f32),
            pltpu.VMEM((n * piece, LANES), f32),
            pltpu.VMEM((n * piece, LANES), f32),
            pltpu.VMEM((dbits * piece, LANES), f32),
            pltpu.VMEM((piece, LANES), f32),
            dma((SLOTS,)), dma, dma((n,)), dma((n,)), dma((n,)), dma((n,)),
            dma((n,)), dma((n,)), dma((n,)), dma((n,)), dma((dbits,)), dma((dbits,)), dma, dma,
        ],
        compiler_params=pltpu.CompilerParams(collective_id=0, has_side_effects=True),
        name="rescore",
    )(ids, counts, queries.reshape(own * tiles, LANES), corpus)
    return logs[:, 0], out


def solution(mesh):
    in_specs = (
        P(("dp", "query"), None),
        P("query", None),
        P(("dp", "query"), None, None),
        P(("dp", "query"), None),
    )
    out_specs = (P("query"), P("query", None))
    return jax.shard_map(body, mesh=mesh, in_specs=in_specs, out_specs=out_specs, check_vma=False)
```

```python
import functools

import jax
import jax.numpy as jnp
from jax import lax
from jax.experimental import pallas as pl
from jax.experimental.pallas import tpu as pltpu
from jax.sharding import PartitionSpec as P

MESH = pl.DeviceIdType.MESH
LANES = 128
SUB = 8
NEG = -1e30
CHUNK = 256
SLOTS = 4


def low_bit(k):
    return (k & -k).bit_length() - 1


def halves_combine(a, b, step, mask):
    u = jnp.where(mask, a, b)
    v = jnp.where(mask, b, a)
    return u + pltpu.roll(v, step, 0)


def sub_reduce(x, op):
    for step in (4, 2, 1):
        x = op(x, pltpu.roll(x, step, 0))
    return x


def kernel(
    cfg, ids, counts, q_hbm, corpus_hbm, out_ref, log_ref,
    c32, stage, allq, acc, core_out, core_in, bits_out, bits_in,
    core_out_stat, core_in_stat, bits_out_stat, bits_in_stat, rx, fin,
    stage_sem, own_sem, ag_send, ag_recv, agc_send, agc_recv,
    rc_send, rc_recv, rb_send, rb_recv, rx_send, rx_recv, fin_send, fin_recv,
):
    n, d, half_rows, slots, tiles, rows, inv_root = cfg
    nbits = n.bit_length() - 1
    dbits = d.bit_length() - 1
    me = lax.axis_index("query")
    dp = lax.axis_index("dp")
    core = lax.rem(dp, 2)
    other = 1 - core
    stat = tiles * SUB
    group_rows = (tiles + 1) * SUB
    groups = half_rows // SUB
    piece = groups * group_rows
    qpiece = half_rows * tiles
    own_lanes = log_ref.shape[1]

    def flip(x, bit):
        return x + (1 << bit) - 2 * (1 << bit) * lax.rem(x // (1 << bit), 2)

    def owner(k):
        s = me
        for b in range(nbits):
            if k >> b & 1:
                s = flip(s, b)
        return s

    def q_to(bit):
        return {"query": flip(me, bit)}

    def d_to(bit):
        return {"dp": flip(dp, bit)}

    barrier = pltpu.get_barrier_semaphore()
    for b in range(nbits):
        pl.semaphore_signal(barrier, inc=1, device_id=q_to(b), device_id_type=MESH)
    for b in range(dbits):
        pl.semaphore_signal(barrier, inc=1, device_id=d_to(b), device_id_type=MESH)

    def stage_copy(i, slot):
        return pltpu.make_async_copy(
            corpus_hbm.at[pl.ds(i * CHUNK, CHUNK), :], stage.at[slot], stage_sem.at[slot]
        )

    for i in range(SLOTS):
        stage_copy(i, i).start()

    def q_at(s, half):
        return pl.multiple_of((s * 2 + half) * qpiece, SUB)

    own_copy = pltpu.make_async_copy(
        q_hbm, allq.at[pl.ds(pl.multiple_of(me * (2 * qpiece), SUB), 2 * qpiece), :], own_sem
    )
    own_copy.start()
    pl.semaphore_wait(barrier, nbits + dbits)

    started = []

    def remote(src, dst, send, recv, to):
        copy = pltpu.make_async_remote_copy(
            src_ref=src, dst_ref=dst, send_sem=send, recv_sem=recv,
            device_id=to, device_id_type=MESH,
        )
        copy.start()
        started.append(copy)
        return copy

    def ag_piece(k, half):
        return allq.at[pl.ds(q_at(owner(k), half), qpiece), :]

    def ag_forward(k):
        for b in reversed(range(low_bit(k) if k else nbits)):
            if k:
                src = ag_piece(k, core)
            else:
                src = q_hbm.at[pl.ds(pl.multiple_of(core * qpiece, SUB), qpiece), :]
            j = k | 1 << b
            remote(src, ag_piece(k, core), ag_send.at[j], ag_recv.at[j], q_to(b))
        if k:
            remote(ag_piece(k, core), ag_piece(k, core), agc_send.at[k], agc_recv.at[k], d_to(0))

    def arrived(k, half, send, recv, to):
        pltpu.make_async_remote_copy(
            src_ref=ag_piece(k, half), dst_ref=ag_piece(k, half), send_sem=send.at[k],
            recv_sem=recv.at[k], device_id=to, device_id_type=MESH,
        ).wait_recv()

    def relay(k):
        arrived(k, core, ag_send, ag_recv, q_to(low_bit(k)))
        ag_forward(k)

    ag_forward(0)

    n_chunks = rows // CHUNK
    flat = c32.reshape(rows * tiles, LANES)

    def convert(i, _):
        slot = lax.rem(i, SLOTS)
        stage_copy(i, slot).wait()

        def block(r, _):
            r0 = pl.multiple_of(r * 16, 16)
            to = pl.multiple_of((i * CHUNK + r * 16) * tiles, SUB)
            for j in range(tiles):
                x = stage[slot, pl.ds(r0, 16), j * LANES : (j + 1) * LANES].astype(jnp.float32)
                flat[pl.ds(to + j, SUB, stride=tiles), :] = x[:SUB]
                flat[pl.ds(to + SUB * tiles + j, SUB, stride=tiles), :] = x[SUB:]
            return 0

        lax.fori_loop(0, CHUNK // 16, block, 0)

        @pl.when(i + SLOTS < n_chunks)
        def _():
            stage_copy(i + SLOTS, slot).start()

        return 0

    relays = sorted(range(1, n), key=lambda k: (k.bit_count(), -low_bit(k), k))
    pending = list(relays)
    parts = 4
    for part in range(parts):
        lax.fori_loop(part * n_chunks // parts, (part + 1) * n_chunks // parts, convert, 0)
        if part and pending:
            relay(pending.pop(0))

    sub = lax.broadcasted_iota(jnp.int32, (SUB, LANES), 0)
    lane = lax.broadcasted_iota(jnp.int32, (SUB, LANES), 1)
    masks = {4: sub < 4, 2: lax.rem(sub, 4) < 2, 1: lax.rem(sub, 2) < 1}

    def acc_at(s, half):
        return pl.multiple_of((s * 2 + half) * piece, SUB)

    def compute(k, half):
        s = owner(k)
        q0 = q_at(s, half)
        a0 = acc_at(s, half)
        first = s * (2 * half_rows) + half * half_rows

        def row(index):
            return c32[ids[index[1], index[0]]]

        def group(g, _):
            query = first + g * SUB
            weights, stats = [], jnp.zeros((SUB, LANES), jnp.float32)
            for qi in range(SUB):
                at = query + qi
                q = allq[pl.ds(pl.multiple_of(q0 + (g * SUB + qi) * tiles, SUB), tiles), :]
                level = [row((at, c)) * q for c in range(slots)]
                for step in (1, 2, 4):
                    level = [
                        halves_combine(a, b, step, masks[step])
                        for a, b in zip(level[::2], level[1::2])
                    ]
                score = jnp.sum(level[0], axis=1, keepdims=True) * inv_root
                score = jnp.broadcast_to(score, (SUB, LANES))
                live = sub < counts[query + qi]
                score = jnp.where(live, score, NEG)
                best = sub_reduce(score, jnp.maximum)
                weight = jnp.where(live, jnp.exp(score - best), 0.0)
                total = sub_reduce(weight, jnp.add)
                weights.append(weight)
                stats = jnp.where(sub == qi, jnp.where(lane < LANES // 2, best, total), stats)
            base = pl.multiple_of(a0 + g * group_rows, SUB)
            for qi in range(SUB):
                at = query + qi
                terms = [
                    jnp.broadcast_to(weights[qi][c : c + 1, :], (SUB, LANES)) * row((at, c))
                    for c in range(slots)
                ]
                while len(terms) > 1:
                    terms = [a + b for a, b in zip(terms[::2], terms[1::2])]
                acc[pl.ds(base + qi, tiles, stride=SUB), :] = terms[0]
            acc[pl.ds(pl.multiple_of(base + stat, SUB), SUB), :] = stats
            return 0

        lax.fori_loop(0, groups, group, 0)

    def split(x):
        turned = pltpu.roll(x, LANES // 2, 1)
        left = lane < LANES // 2
        return jnp.where(left, x, turned), jnp.where(left, turned, x)

    def merge(k, ref, at, swap=None):
        a0 = acc_at(owner(k), core)

        def group(g, _):
            mine = pl.multiple_of(a0 + g * group_rows, SUB)
            theirs = pl.multiple_of(at + g * group_rows, SUB)

            def load(off):
                x = acc[pl.ds(pl.multiple_of(mine + off, SUB), SUB), :]
                y = ref[pl.ds(pl.multiple_of(theirs + off, SUB), SUB), :]
                if swap is not None:
                    x, y = jnp.where(swap, y, x), jnp.where(swap, x, y)
                return x, y

            x, y = load(stat)
            best_x, total_x = split(x)
            best_y, total_y = split(y)
            best = jnp.maximum(best_x, best_y)
            scale_x = jnp.exp(best_x - best)
            scale_y = jnp.exp(best_y - best)
            total = total_x * scale_x + total_y * scale_y
            acc[pl.ds(pl.multiple_of(mine + stat, SUB), SUB), :] = jnp.where(
                lane < LANES // 2, best, total
            )
            for j in range(tiles):
                x, y = load(j * SUB)
                acc[pl.ds(pl.multiple_of(mine + j * SUB, SUB), SUB), :] = x * scale_x + y * scale_y
            return 0

        lax.fori_loop(0, groups, group, 0)

    fields = 3
    field_lanes = LANES // (groups * fields)
    prow = half_rows * tiles

    def pack(k, half, data, stats):
        a0 = acc_at(owner(k), half)

        def group(g, packed):
            base = pl.multiple_of(a0 + g * group_rows, SUB)
            values = [acc[pl.ds(pl.multiple_of(base + j * SUB, SUB), SUB), :] for j in range(tiles)]
            best, total = split(acc[pl.ds(pl.multiple_of(base + stat, SUB), SUB), :])
            largest = functools.reduce(jnp.maximum, [jnp.abs(v) for v in values])
            largest = jnp.maximum(jnp.max(largest, axis=1, keepdims=True), 1e-30)
            largest = jnp.broadcast_to(largest, (SUB, LANES))
            inverse = 32767.0 / largest
            for j in range(0, tiles, 2):
                x = jnp.concatenate([values[j] * inverse, values[j + 1] * inverse], axis=0)
                at = pl.multiple_of(k * prow + g * (tiles * SUB) + j * SUB, 2 * SUB)
                data[pl.ds(at, 2 * SUB), :] = jnp.round(x).astype(jnp.int32).astype(jnp.int16)
            for f, x in enumerate((best, total, largest)):
                packed = jnp.where(lane // field_lanes == g * fields + f, x, packed)
            return packed

        packed = lax.fori_loop(0, groups, group, jnp.zeros((SUB, LANES), jnp.float32))
        stats[pl.ds(k * SUB, SUB), :] = packed

    def merge_packed(k, data, stats, j_in):
        a0 = acc_at(owner(k), core)
        packed = stats[pl.ds(j_in * SUB, SUB), :]

        def group(g, _):
            base = pl.multiple_of(a0 + g * group_rows, SUB)

            def field(f):
                x = jnp.where(lane == (g * fields + f) * field_lanes, packed, 0.0)
                return jnp.broadcast_to(jnp.sum(x, axis=1, keepdims=True), (SUB, LANES))

            best_x, total_x = split(acc[pl.ds(pl.multiple_of(base + stat, SUB), SUB), :])
            best_y, total_y, largest = field(0), field(1), field(2)
            best = jnp.maximum(best_x, best_y)
            scale_x = jnp.exp(best_x - best)
            scale_y = jnp.exp(best_y - best)
            total = total_x * scale_x + total_y * scale_y
            acc[pl.ds(pl.multiple_of(base + stat, SUB), SUB), :] = jnp.where(
                lane < LANES // 2, best, total
            )
            step_y = largest * (1.0 / 32767.0) * scale_y
            for j in range(0, tiles, 2):
                at = pl.multiple_of(j_in * prow + g * (tiles * SUB) + j * SUB, 2 * SUB)
                y = data[pl.ds(at, 2 * SUB), :].astype(jnp.int32).astype(jnp.float32)
                for i in range(2):
                    to = pl.ds(pl.multiple_of(base + (j + i) * SUB, SUB), SUB)
                    acc[to, :] = acc[to, :] * scale_x + y[i * SUB : (i + 1) * SUB] * step_y
            return 0

        lax.fori_loop(0, groups, group, 0)

    def pair(k, source, source_stat, target, target_stat, send, recv, to):
        rows_of, tile_of = pl.ds(k * prow, prow), pl.ds(k * SUB, SUB)
        return (
            pltpu.make_async_remote_copy(
                src_ref=source.at[rows_of, :], dst_ref=target.at[rows_of, :],
                send_sem=send.at[k], recv_sem=recv.at[k], device_id=to, device_id_type=MESH,
            ),
            pltpu.make_async_remote_copy(
                src_ref=source_stat.at[tile_of, :], dst_ref=target_stat.at[tile_of, :],
                send_sem=send.at[n + k], recv_sem=recv.at[n + k], device_id=to, device_id_type=MESH,
            ),
        )

    def core_pair(k):
        return pair(k, core_out, core_out_stat, core_in, core_in_stat, rc_send, rc_recv, d_to(0))

    def bits_pair(k):
        return pair(
            k, bits_out, bits_out_stat, bits_in, bits_in_stat, rb_send, rb_recv, q_to(low_bit(k))
        )

    def launch(copies):
        for copy in copies:
            copy.start()
            started.append(copy)

    def acc_piece(k, half):
        return acc.at[pl.ds(acc_at(owner(k), half), piece), :]

    def slot_of(ref, k):
        return ref.at[pl.ds(k * piece, piece), :]

    def share(k):
        pack(k, other, core_out, core_out_stat)
        launch(core_pair(k))

    def finish(k):
        for copy in core_pair(k):
            copy.wait_recv()
        merge_packed(k, core_in, core_in_stat, k)
        for b in range(low_bit(k) if k else nbits):
            j = k | 1 << b
            for copy in bits_pair(j):
                copy.wait_recv()
            merge_packed(k, bits_in, bits_in_stat, j)
        if k:
            pack(k, core, bits_out, bits_out_stat)
            launch(bits_pair(k))

    order = [0] + sorted(range(1, n), key=lambda k: (low_bit(k), k.bit_count(), k))
    own_copy.wait()
    late = None
    for k in order:
        while k and k in pending:
            relay(pending.pop(0))
        if k:
            arrived(k, other, agc_send, agc_recv, d_to(0))
        compute(k, other)
        share(k)
        compute(k, core)
        if late:
            finish(late)
        late = k
    finish(late)
    finish(0)

    for b in range(1, dbits):
        pltpu_copy = pltpu.make_async_remote_copy(
            src_ref=acc_piece(0, core), dst_ref=slot_of(rx, b), send_sem=rx_send.at[b],
            recv_sem=rx_recv.at[b], device_id=d_to(b), device_id_type=MESH,
        )
        pltpu_copy.start()
        pltpu_copy.wait()
        upper = jnp.full((SUB, LANES), lax.rem(dp // (1 << b), 2), jnp.int32)
        merge(0, rx, b * piece, swap=upper == 1)

    last = remote(acc_piece(0, core), fin, fin_send, fin_recv, d_to(0))

    logs = []
    wide = lax.broadcasted_iota(jnp.int32, (SUB, own_lanes), 1)
    deep = lax.broadcasted_iota(jnp.int32, (SUB, own_lanes), 0)

    def emit(ref, at, half):
        for g in range(groups):
            base = pl.multiple_of(at + g * group_rows, SUB)
            to = pl.multiple_of(half * half_rows + g * SUB, SUB)
            best, total = split(ref[pl.ds(pl.multiple_of(base + stat, SUB), SUB), :])
            value = (best + jnp.log(total))[:, :1]
            logs.append(jnp.where(wide == to + deep, value, 0.0))
            inverse = 1.0 / total
            for j in range(tiles):
                out_ref[pl.ds(to, SUB), j * LANES : (j + 1) * LANES] = (
                    ref[pl.ds(pl.multiple_of(base + j * SUB, SUB), SUB), :] * inverse
                )

    emit(acc, acc_at(me, core), core)
    last.wait_recv()
    emit(fin, 0, other)
    log_ref[...] = jnp.sum(functools.reduce(jnp.add, logs), axis=0, keepdims=True)
    for copy in started:
        copy.wait_send()


def body(corpus, queries, cand_ids, cand_counts):
    n, d = lax.axis_size("query"), lax.axis_size("dp")
    own, width = queries.shape
    slots = cand_ids.shape[2]
    rows = corpus.shape[0]
    tiles = width // LANES
    half_rows = own // 2
    inv_root = 1.0 / float(width) ** 0.5
    ids = cand_ids[0].T
    counts = cand_counts.reshape(-1)
    piece = half_rows // SUB * (tiles + 1) * SUB
    qpiece = half_rows * tiles
    dbits = d.bit_length() - 1
    f32 = jnp.float32
    dma = pltpu.SemaphoreType.DMA
    out, logs = pl.pallas_call(
        functools.partial(kernel, (n, d, half_rows, slots, tiles, rows, inv_root)),
        out_shape=(
            jax.ShapeDtypeStruct((own, width), f32),
            jax.ShapeDtypeStruct((1, own), f32),
        ),
        in_specs=[
            pl.BlockSpec(memory_space=pltpu.SMEM),
            pl.BlockSpec(memory_space=pltpu.SMEM),
            pl.BlockSpec(memory_space=pl.ANY),
            pl.BlockSpec(memory_space=pl.ANY),
        ],
        out_specs=(pl.BlockSpec(memory_space=pltpu.VMEM), pl.BlockSpec(memory_space=pltpu.VMEM)),
        scratch_shapes=[
            pltpu.VMEM((rows, tiles, LANES), f32),
            pltpu.VMEM((SLOTS, CHUNK, width), corpus.dtype),
            pltpu.VMEM((n * 2 * qpiece, LANES), f32),
            pltpu.VMEM((n * 2 * piece, LANES), f32),
            *[pltpu.VMEM((n * qpiece, LANES), jnp.int16)] * 4,
            *[pltpu.VMEM((n * SUB, LANES), f32)] * 4,
            pltpu.VMEM((dbits * piece, LANES), f32),
            pltpu.VMEM((piece, LANES), f32),
            dma((SLOTS,)), dma, dma((n,)), dma((n,)), dma((n,)), dma((n,)),
            *[dma((2 * n,))] * 4, dma((dbits,)), dma((dbits,)), dma, dma,
        ],
        compiler_params=pltpu.CompilerParams(collective_id=0, has_side_effects=True),
        name="rescore",
    )(ids, counts, queries.reshape(own * tiles, LANES), corpus)
    return logs[0], out


def solution(mesh):
    in_specs = (
        P(("dp", "query"), None),
        P("query", None),
        P(("dp", "query"), None, None),
        P(("dp", "query"), None),
    )
    out_specs = (P("query"), P("query", None))
    return jax.shard_map(body, mesh=mesh, in_specs=in_specs, out_specs=out_specs, check_vma=False)
```

```python
import functools

import jax
import jax.numpy as jnp
from jax import lax
from jax.experimental import pallas as pl
from jax.experimental.pallas import tpu as pltpu
from jax.sharding import PartitionSpec as P

MESH = pl.DeviceIdType.MESH
LANES = 128
SUB = 8
NEG = -1e30
CHUNK = 256
SLOTS = 4


def low_bit(k):
    return (k & -k).bit_length() - 1


def halves_combine(a, b, step, mask):
    u = jnp.where(mask, a, b)
    v = jnp.where(mask, b, a)
    return u + pltpu.roll(v, step, 0)


def sub_reduce(x, op):
    for step in (4, 2, 1):
        x = op(x, pltpu.roll(x, step, 0))
    return x


def kernel(
    cfg, ids, counts, q_hbm, corpus_hbm, out_ref, log_ref,
    c32, stage, allq, acc, core_out, core_in, bits_out, bits_in,
    core_out_stat, core_in_stat, bits_out_stat, bits_in_stat, rx, fin,
    stage_sem, own_sem, ag_send, ag_recv, agc_send, agc_recv,
    rc_send, rc_recv, rb_send, rb_recv, rx_send, rx_recv, fin_send, fin_recv,
):
    n, d, half_rows, slots, tiles, rows, inv_root = cfg
    nbits = n.bit_length() - 1
    dbits = d.bit_length() - 1
    me = lax.axis_index("query")
    dp = lax.axis_index("dp")
    core = lax.rem(dp, 2)
    other = 1 - core
    stat = tiles * SUB
    group_rows = (tiles + 1) * SUB
    groups = half_rows // SUB
    piece = groups * group_rows
    qpiece = half_rows * tiles
    own_lanes = log_ref.shape[1]

    def flip(x, bit):
        return x + (1 << bit) - 2 * (1 << bit) * lax.rem(x // (1 << bit), 2)

    def owner(k):
        s = me
        for b in range(nbits):
            if k >> b & 1:
                s = flip(s, b)
        return s

    def q_to(bit):
        return {"query": flip(me, bit)}

    def d_to(bit):
        return {"dp": flip(dp, bit)}

    barrier = pltpu.get_barrier_semaphore()
    for b in range(nbits):
        pl.semaphore_signal(barrier, inc=1, device_id=q_to(b), device_id_type=MESH)
    for b in range(dbits):
        pl.semaphore_signal(barrier, inc=1, device_id=d_to(b), device_id_type=MESH)

    def stage_copy(i, slot):
        return pltpu.make_async_copy(
            corpus_hbm.at[pl.ds(i * CHUNK, CHUNK), :], stage.at[slot], stage_sem.at[slot]
        )

    for i in range(SLOTS):
        stage_copy(i, i).start()

    def q_at(s, half):
        return pl.multiple_of((s * 2 + half) * qpiece, SUB)

    own_copy = pltpu.make_async_copy(
        q_hbm, allq.at[pl.ds(pl.multiple_of(me * (2 * qpiece), SUB), 2 * qpiece), :], own_sem
    )
    own_copy.start()
    pl.semaphore_wait(barrier, nbits + dbits)

    started = []

    def remote(src, dst, send, recv, to):
        copy = pltpu.make_async_remote_copy(
            src_ref=src, dst_ref=dst, send_sem=send, recv_sem=recv,
            device_id=to, device_id_type=MESH,
        )
        copy.start()
        started.append(copy)
        return copy

    def ag_piece(k, half):
        return allq.at[pl.ds(q_at(owner(k), half), qpiece), :]

    def ag_forward(k):
        for b in reversed(range(low_bit(k) if k else nbits)):
            if k:
                src = ag_piece(k, core)
            else:
                src = q_hbm.at[pl.ds(pl.multiple_of(core * qpiece, SUB), qpiece), :]
            j = k | 1 << b
            remote(src, ag_piece(k, core), ag_send.at[j], ag_recv.at[j], q_to(b))
        if k:
            remote(ag_piece(k, core), ag_piece(k, core), agc_send.at[k], agc_recv.at[k], d_to(0))

    def arrived(k, half, send, recv, to):
        pltpu.make_async_remote_copy(
            src_ref=ag_piece(k, half), dst_ref=ag_piece(k, half), send_sem=send.at[k],
            recv_sem=recv.at[k], device_id=to, device_id_type=MESH,
        ).wait_recv()

    def relay(k):
        arrived(k, core, ag_send, ag_recv, q_to(low_bit(k)))
        ag_forward(k)

    ag_forward(0)

    n_chunks = rows // CHUNK
    flat = c32.reshape(rows * tiles, LANES)

    def convert(i, _):
        slot = lax.rem(i, SLOTS)
        stage_copy(i, slot).wait()

        def block(r, _):
            r0 = pl.multiple_of(r * 16, 16)
            to = pl.multiple_of((i * CHUNK + r * 16) * tiles, SUB)
            for j in range(tiles):
                x = stage[slot, pl.ds(r0, 16), j * LANES : (j + 1) * LANES].astype(jnp.float32)
                flat[pl.ds(to + j, SUB, stride=tiles), :] = x[:SUB]
                flat[pl.ds(to + SUB * tiles + j, SUB, stride=tiles), :] = x[SUB:]
            return 0

        lax.fori_loop(0, CHUNK // 16, block, 0)

        @pl.when(i + SLOTS < n_chunks)
        def _():
            stage_copy(i + SLOTS, slot).start()

        return 0

    relays = sorted(range(1, n), key=lambda k: (k.bit_count(), -low_bit(k), k))
    pending = list(relays)
    parts = 4
    for part in range(parts):
        lax.fori_loop(part * n_chunks // parts, (part + 1) * n_chunks // parts, convert, 0)
        if part and pending:
            relay(pending.pop(0))

    sub = lax.broadcasted_iota(jnp.int32, (SUB, LANES), 0)
    lane = lax.broadcasted_iota(jnp.int32, (SUB, LANES), 1)
    masks = {4: sub < 4, 2: lax.rem(sub, 4) < 2, 1: lax.rem(sub, 2) < 1}

    def acc_at(s, half):
        return pl.multiple_of((s * 2 + half) * piece, SUB)

    def compute(k, half):
        s = owner(k)
        q0 = q_at(s, half)
        a0 = acc_at(s, half)
        first = s * (2 * half_rows) + half * half_rows

        def row(index):
            return c32[ids[index[1], index[0]]]

        def group(g, _):
            query = first + g * SUB
            weights, stats = [], jnp.zeros((SUB, LANES), jnp.float32)
            for qi in range(SUB):
                at = query + qi
                q = allq[pl.ds(pl.multiple_of(q0 + (g * SUB + qi) * tiles, SUB), tiles), :]
                level = [row((at, c)) * q for c in range(slots)]
                for step in (1, 2, 4):
                    level = [
                        halves_combine(a, b, step, masks[step])
                        for a, b in zip(level[::2], level[1::2])
                    ]
                score = jnp.sum(level[0], axis=1, keepdims=True) * inv_root
                score = jnp.broadcast_to(score, (SUB, LANES))
                live = sub < counts[query + qi]
                score = jnp.where(live, score, NEG)
                best = sub_reduce(score, jnp.maximum)
                weight = jnp.where(live, jnp.exp(score - best), 0.0)
                total = sub_reduce(weight, jnp.add)
                weights.append(weight)
                stats = jnp.where(sub == qi, jnp.where(lane < LANES // 2, best, total), stats)
            base = pl.multiple_of(a0 + g * group_rows, SUB)
            for qi in range(SUB):
                at = query + qi
                terms = [
                    jnp.broadcast_to(weights[qi][c : c + 1, :], (SUB, LANES)) * row((at, c))
                    for c in range(slots)
                ]
                while len(terms) > 1:
                    terms = [a + b for a, b in zip(terms[::2], terms[1::2])]
                acc[pl.ds(base + qi, tiles, stride=SUB), :] = terms[0]
            acc[pl.ds(pl.multiple_of(base + stat, SUB), SUB), :] = stats
            return 0

        lax.fori_loop(0, groups, group, 0, unroll=2)

    def split(x):
        turned = pltpu.roll(x, LANES // 2, 1)
        left = lane < LANES // 2
        return jnp.where(left, x, turned), jnp.where(left, turned, x)

    def merge(k, ref, at, swap=None):
        a0 = acc_at(owner(k), core)

        def group(g, _):
            mine = pl.multiple_of(a0 + g * group_rows, SUB)
            theirs = pl.multiple_of(at + g * group_rows, SUB)

            def load(off):
                x = acc[pl.ds(pl.multiple_of(mine + off, SUB), SUB), :]
                y = ref[pl.ds(pl.multiple_of(theirs + off, SUB), SUB), :]
                if swap is not None:
                    x, y = jnp.where(swap, y, x), jnp.where(swap, x, y)
                return x, y

            x, y = load(stat)
            best_x, total_x = split(x)
            best_y, total_y = split(y)
            best = jnp.maximum(best_x, best_y)
            scale_x = jnp.exp(best_x - best)
            scale_y = jnp.exp(best_y - best)
            total = total_x * scale_x + total_y * scale_y
            acc[pl.ds(pl.multiple_of(mine + stat, SUB), SUB), :] = jnp.where(
                lane < LANES // 2, best, total
            )
            for j in range(tiles):
                x, y = load(j * SUB)
                acc[pl.ds(pl.multiple_of(mine + j * SUB, SUB), SUB), :] = x * scale_x + y * scale_y
            return 0

        lax.fori_loop(0, groups, group, 0, unroll=True)

    fields = 3
    field_lanes = LANES // (groups * fields)
    prow = half_rows * tiles

    def pack(k, half, data, stats):
        a0 = acc_at(owner(k), half)

        def group(g, packed):
            base = pl.multiple_of(a0 + g * group_rows, SUB)
            values = [acc[pl.ds(pl.multiple_of(base + j * SUB, SUB), SUB), :] for j in range(tiles)]
            best, total = split(acc[pl.ds(pl.multiple_of(base + stat, SUB), SUB), :])
            largest = functools.reduce(jnp.maximum, [jnp.abs(v) for v in values])
            largest = jnp.maximum(jnp.max(largest, axis=1, keepdims=True), 1e-30)
            largest = jnp.broadcast_to(largest, (SUB, LANES))
            inverse = 32767.0 / largest
            for j in range(0, tiles, 2):
                x = jnp.concatenate([values[j] * inverse, values[j + 1] * inverse], axis=0)
                at = pl.multiple_of(k * prow + g * (tiles * SUB) + j * SUB, 2 * SUB)
                data[pl.ds(at, 2 * SUB), :] = jnp.round(x).astype(jnp.int32).astype(jnp.int16)
            for f, x in enumerate((best, total, largest)):
                packed = jnp.where(lane // field_lanes == g * fields + f, x, packed)
            return packed

        packed = lax.fori_loop(0, groups, group, jnp.zeros((SUB, LANES), jnp.float32), unroll=True)
        stats[pl.ds(k * SUB, SUB), :] = packed

    def merge_packed(k, data, stats, j_in):
        a0 = acc_at(owner(k), core)
        packed = stats[pl.ds(j_in * SUB, SUB), :]

        def group(g, _):
            base = pl.multiple_of(a0 + g * group_rows, SUB)

            def field(f):
                x = jnp.where(lane == (g * fields + f) * field_lanes, packed, 0.0)
                return jnp.broadcast_to(jnp.sum(x, axis=1, keepdims=True), (SUB, LANES))

            best_x, total_x = split(acc[pl.ds(pl.multiple_of(base + stat, SUB), SUB), :])
            best_y, total_y, largest = field(0), field(1), field(2)
            best = jnp.maximum(best_x, best_y)
            scale_x = jnp.exp(best_x - best)
            scale_y = jnp.exp(best_y - best)
            total = total_x * scale_x + total_y * scale_y
            acc[pl.ds(pl.multiple_of(base + stat, SUB), SUB), :] = jnp.where(
                lane < LANES // 2, best, total
            )
            step_y = largest * (1.0 / 32767.0) * scale_y
            for j in range(0, tiles, 2):
                at = pl.multiple_of(j_in * prow + g * (tiles * SUB) + j * SUB, 2 * SUB)
                y = data[pl.ds(at, 2 * SUB), :].astype(jnp.int32).astype(jnp.float32)
                for i in range(2):
                    to = pl.ds(pl.multiple_of(base + (j + i) * SUB, SUB), SUB)
                    acc[to, :] = acc[to, :] * scale_x + y[i * SUB : (i + 1) * SUB] * step_y
            return 0

        lax.fori_loop(0, groups, group, 0, unroll=True)

    def pair(k, source, source_stat, target, target_stat, send, recv, to):
        rows_of, tile_of = pl.ds(k * prow, prow), pl.ds(k * SUB, SUB)
        return (
            pltpu.make_async_remote_copy(
                src_ref=source.at[rows_of, :], dst_ref=target.at[rows_of, :],
                send_sem=send.at[k], recv_sem=recv.at[k], device_id=to, device_id_type=MESH,
            ),
            pltpu.make_async_remote_copy(
                src_ref=source_stat.at[tile_of, :], dst_ref=target_stat.at[tile_of, :],
                send_sem=send.at[n + k], recv_sem=recv.at[n + k], device_id=to, device_id_type=MESH,
            ),
        )

    def core_pair(k):
        return pair(k, core_out, core_out_stat, core_in, core_in_stat, rc_send, rc_recv, d_to(0))

    def bits_pair(k):
        return pair(
            k, bits_out, bits_out_stat, bits_in, bits_in_stat, rb_send, rb_recv, q_to(low_bit(k))
        )

    def launch(copies):
        for copy in copies:
            copy.start()
            started.append(copy)

    def acc_piece(k, half):
        return acc.at[pl.ds(acc_at(owner(k), half), piece), :]

    def slot_of(ref, k):
        return ref.at[pl.ds(k * piece, piece), :]

    def share(k):
        pack(k, other, core_out, core_out_stat)
        launch(core_pair(k))

    def finish(k):
        for copy in core_pair(k):
            copy.wait_recv()
        merge_packed(k, core_in, core_in_stat, k)
        for b in range(low_bit(k) if k else nbits):
            j = k | 1 << b
            for copy in bits_pair(j):
                copy.wait_recv()
            merge_packed(k, bits_in, bits_in_stat, j)
        if k:
            pack(k, core, bits_out, bits_out_stat)
            launch(bits_pair(k))

    order = [0] + sorted(range(1, n), key=lambda k: (low_bit(k), k.bit_count(), k))
    own_copy.wait()
    late = None
    for k in order:
        while k and k in pending:
            relay(pending.pop(0))
        if k:
            arrived(k, other, agc_send, agc_recv, d_to(0))
        compute(k, other)
        share(k)
        if late:
            finish(late)
        compute(k, core)
        late = k
    finish(late)
    finish(0)

    for b in range(1, dbits):
        pltpu_copy = pltpu.make_async_remote_copy(
            src_ref=acc_piece(0, core), dst_ref=slot_of(rx, b), send_sem=rx_send.at[b],
            recv_sem=rx_recv.at[b], device_id=d_to(b), device_id_type=MESH,
        )
        pltpu_copy.start()
        pltpu_copy.wait()
        upper = jnp.full((SUB, LANES), lax.rem(dp // (1 << b), 2), jnp.int32)
        merge(0, rx, b * piece, swap=upper == 1)

    last = remote(acc_piece(0, core), fin, fin_send, fin_recv, d_to(0))

    logs = []
    wide = lax.broadcasted_iota(jnp.int32, (SUB, own_lanes), 1)
    deep = lax.broadcasted_iota(jnp.int32, (SUB, own_lanes), 0)

    def emit(ref, at, half):
        for g in range(groups):
            base = pl.multiple_of(at + g * group_rows, SUB)
            to = pl.multiple_of(half * half_rows + g * SUB, SUB)
            best, total = split(ref[pl.ds(pl.multiple_of(base + stat, SUB), SUB), :])
            value = (best + jnp.log(total))[:, :1]
            logs.append(jnp.where(wide == to + deep, value, 0.0))
            inverse = 1.0 / total
            for j in range(tiles):
                out_ref[pl.ds(to, SUB), j * LANES : (j + 1) * LANES] = (
                    ref[pl.ds(pl.multiple_of(base + j * SUB, SUB), SUB), :] * inverse
                )

    emit(acc, acc_at(me, core), core)
    last.wait_recv()
    emit(fin, 0, other)
    log_ref[...] = jnp.sum(functools.reduce(jnp.add, logs), axis=0, keepdims=True)
    for copy in started:
        copy.wait_send()


def body(corpus, queries, cand_ids, cand_counts):
    n, d = lax.axis_size("query"), lax.axis_size("dp")
    own, width = queries.shape
    slots = cand_ids.shape[2]
    rows = corpus.shape[0]
    tiles = width // LANES
    half_rows = own // 2
    inv_root = 1.0 / float(width) ** 0.5
    ids = cand_ids[0].T
    counts = cand_counts.reshape(-1)
    piece = half_rows // SUB * (tiles + 1) * SUB
    qpiece = half_rows * tiles
    dbits = d.bit_length() - 1
    f32 = jnp.float32
    dma = pltpu.SemaphoreType.DMA
    out, logs = pl.pallas_call(
        functools.partial(kernel, (n, d, half_rows, slots, tiles, rows, inv_root)),
        out_shape=(
            jax.ShapeDtypeStruct((own, width), f32),
            jax.ShapeDtypeStruct((1, own), f32),
        ),
        in_specs=[
            pl.BlockSpec(memory_space=pltpu.SMEM),
            pl.BlockSpec(memory_space=pltpu.SMEM),
            pl.BlockSpec(memory_space=pl.ANY),
            pl.BlockSpec(memory_space=pl.ANY),
        ],
        out_specs=(pl.BlockSpec(memory_space=pltpu.VMEM), pl.BlockSpec(memory_space=pltpu.VMEM)),
        scratch_shapes=[
            pltpu.VMEM((rows, tiles, LANES), f32),
            pltpu.VMEM((SLOTS, CHUNK, width), corpus.dtype),
            pltpu.VMEM((n * 2 * qpiece, LANES), f32),
            pltpu.VMEM((n * 2 * piece, LANES), f32),
            *[pltpu.VMEM((n * qpiece, LANES), jnp.int16)] * 4,
            *[pltpu.VMEM((n * SUB, LANES), f32)] * 4,
            pltpu.VMEM((dbits * piece, LANES), f32),
            pltpu.VMEM((piece, LANES), f32),
            dma((SLOTS,)), dma, dma((n,)), dma((n,)), dma((n,)), dma((n,)),
            *[dma((2 * n,))] * 4, dma((dbits,)), dma((dbits,)), dma, dma,
        ],
        compiler_params=pltpu.CompilerParams(collective_id=0, has_side_effects=True),
        name="rescore",
    )(ids, counts, queries.reshape(own * tiles, LANES), corpus)
    return logs[0], out


def solution(mesh):
    in_specs = (
        P(("dp", "query"), None),
        P("query", None),
        P(("dp", "query"), None, None),
        P(("dp", "query"), None),
    )
    out_specs = (P("query"), P("query", None))
    return jax.shard_map(body, mesh=mesh, in_specs=in_specs, out_specs=out_specs, check_vma=False)
```
